32 devices in a mesh: sector: 8 (over z, core), term: 4 (over y, x).
Axes of the slice: x: 2, y: 2, z: 4, core: 2. Of those that a mesh axis runs over, the one named last changes fastest.
Arguments:
- psi: bfloat16 [128, 256, 256], P('sector'), may hold values from -6 to 6
- sector_sizes: int32 [128], P('sector'), may hold values from 64 to 256, as said below
- left_env: bfloat16 [192, 8, 256, 256], P('term', 'sector'), may hold values from -0.109375 to 0.109375
- right_env: bfloat16 [192, 8, 256, 256], P('term', 'sector'), may hold values from -0.375 to 0.375
- target: int32 [192, 8], P('term', 'sector'), may hold values from 0 to 127, as said below
- source: int32 [192, 8], P('term', 'sector'), may hold values from 0 to 127, as said below
- live_count: int32 [4, 8], P('term', 'sector'), may hold values from 1 to 48, as said below
Outputs:
- sigma: float32 [128, 256, 256], P('sector', 'term')
The draws below stay inside these ranges and needn't reach their ends.
Inputs may be any that keep to these rules, and one draw needn't show every extreme that they name: target[j, g] lies among the sectors of sector group g, from g * 16 to (g + 1) * 16 - 1. source[j, g] differs from target[j, g] by at most 16. `live_count`: some device has all 48 slots live in every draw. `sector_sizes`: some sector has all 256 rows live in every draw.
All inputs are finite; a program needn't handle non-finite values.
Results may differ from the reference program's by a relative error of at most 0.0042.
Values may be sent and summed in bfloat16 or wider, within the bound.
A program may use at most 128 MiB of HBM per device.

```python
import jax
import jax.numpy as jnp
from jax import lax

M = 256
SEC_DEV = 16
SLOT_DEV = 48
SECTORS = 128
GROUPS = 8
TGROUPS = 4
SLOTS = 192


def pair_plan(key):
    base = jax.random.fold_in(key, 7)
    offset = jax.random.randint(jax.random.fold_in(base, 1), (SLOTS, GROUPS), 0, SEC_DEV)
    groups_iota = jnp.arange(GROUPS, dtype=jnp.int32)[None, :]
    target_ids = (groups_iota * SEC_DEV + offset).astype(jnp.int32)
    moved = jax.random.randint(jax.random.fold_in(base, 2), (SLOTS, GROUPS), -SEC_DEV, SEC_DEV + 1)
    source_ids = jnp.clip(target_ids + moved, 0, SECTORS - 1).astype(jnp.int32)
    return (target_ids, source_ids)


def draw_target(key, part):
    return pair_plan(key)[0]


def draw_source(key, part):
    return pair_plan(key)[1]


def draw_live_count(key, part):
    base = jax.random.fold_in(key, 11)
    counts = jax.random.randint(jax.random.fold_in(base, 1), (TGROUPS * GROUPS,), 1, SLOT_DEV + 1)
    spot = jax.random.randint(jax.random.fold_in(base, 2), (), 0, TGROUPS * GROUPS)
    counts = jnp.where(jnp.arange(TGROUPS * GROUPS) == spot, SLOT_DEV, counts)
    return counts.reshape(TGROUPS, GROUPS).astype(jnp.int32)


def draw_sector_sizes(key, part):
    base = jax.random.fold_in(key, 13)
    sizes_drawn = jax.random.randint(jax.random.fold_in(base, 1), (SECTORS,), M // 4, M + 1)
    spot = jax.random.randint(jax.random.fold_in(base, 2), (), 0, SECTORS)
    sizes_drawn = jnp.where(jnp.arange(SECTORS) == spot, M, sizes_drawn)
    return sizes_drawn.astype(jnp.int32)


def levels(own_key, dims, pieces, least, top_value):
    level = 1.0
    for dim, parts in pieces:
        draws = jax.random.uniform(jax.random.fold_in(jax.random.fold_in(own_key, 6), dim), (parts,), jnp.float32, least / len(pieces), top_value / len(pieces))
        level = level * jnp.repeat(jnp.exp(draws), dims[dim] // parts).reshape((-1,) + (1,) * (len(dims) - 1 - dim))
    return level


def normal_values(own_key, shape, spread, most, shards=(), held_as=jnp.bfloat16):
    values = spread * jax.random.normal(own_key, shape, jnp.float32)
    if shards:
        values = values * levels(own_key, shape, shards, -0.22, 0.18)
    return jnp.clip(values, -most, most).astype(held_as)


def setup_inputs(seed: int = 0) -> dict:
    arg_keys = jax.random.split(jax.random.key(seed), 8)
    return {
        "psi": normal_values(arg_keys[0], (SECTORS, M, M), 1.0, 6.0, ((0, 8),)),
        "sector_sizes": draw_sector_sizes(jax.random.fold_in(arg_keys[7], 71), 0),
        "left_env": normal_values(arg_keys[2], (SLOTS, GROUPS, M, M), (M * SLOTS // SEC_DEV) ** -0.5, 0.109375, ((0, 4), (1, 8))),
        "right_env": normal_values(arg_keys[3], (SLOTS, GROUPS, M, M), M ** -0.5, 0.375, ((0, 4), (1, 8))),
        "target": draw_target(jax.random.fold_in(arg_keys[7], 71), 0),
        "source": draw_source(jax.random.fold_in(arg_keys[7], 71), 0),
        "live_count": draw_live_count(jax.random.fold_in(arg_keys[7], 71), 0),
    }


def reference(psi, sector_sizes, left_env, right_env, target, source, live_count):
    index_row = jnp.arange(M, dtype=jnp.int32)
    keep = (index_row[None, :, None] < sector_sizes[:, None, None]) & (index_row[None, None, :] < sector_sizes[:, None, None])
    masked = jnp.where(keep, psi, jnp.zeros_like(psi))
    slot_ids = jnp.arange(SLOTS, dtype=jnp.int32)

    def visit(carry, inputs):
        left, right, tgt, src, slot = inputs
        picked = masked[src].astype(jnp.float32)
        inner = jnp.einsum("gab,gbc->gac", left.astype(jnp.float32), picked, precision=lax.Precision.HIGHEST).astype(jnp.bfloat16)
        contribution = jnp.einsum("gac,gdc->gad", inner.astype(jnp.float32), right.astype(jnp.float32), precision=lax.Precision.HIGHEST)
        alive = (slot % SLOT_DEV) < live_count[slot // SLOT_DEV]
        contribution = contribution * alive.astype(jnp.float32)[:, None, None]
        return carry.at[tgt].add(contribution), None

    start = jnp.zeros((SECTORS, M, M), jnp.float32)
    total, unused = lax.scan(visit, start, (left_env, right_env, target, source, slot_ids))
    return jnp.where(keep, total, jnp.zeros_like(total))
```

```python
import functools
import math

import jax
import jax.numpy as jnp
from jax import lax
from jax.experimental import pallas as pl
from jax.experimental.pallas import tpu as pltpu
from jax.sharding import PartitionSpec as P

MESH = pl.DeviceIdType.MESH
RS_GROUPS = 4
UNROLL = 4


def kernel(
    terms, groups,
    order_ref, ends_ref, sizes_ref, psi_ref, left_ref, right_ref,
    out_ref,
    nearby, left, right, running, outgoing, incoming, own,
    load_sems, near_send, near_recv, far_send, far_recv, pass_send, pass_recv, sum_send, sum_recv,
):
    secs, block = psi_ref.shape[0], psi_ref.shape[1]
    slots = left_ref.shape[0]
    rows = block // terms
    side = math.isqrt(terms)
    quarter = secs // 4
    group, term = lax.axis_index("sector"), lax.axis_index("term")
    odd = lax.rem(group, 2)
    near = group + 1 - 2 * odd
    far = group - 1 + 2 * odd
    has_far = jnp.logical_and(far >= 0, far < groups)
    col, row = lax.rem(term, side), lax.div(term, side)
    odd_col, odd_row = lax.rem(col, 2), lax.rem(row, 2)
    col_mate = term + 1 - 2 * odd_col
    row_mate = term + (1 - 2 * odd_row) * side

    psi_load = pltpu.make_async_copy(psi_ref, nearby.at[pl.ds(0, secs)], load_sems.at[0])
    left_load = pltpu.make_async_copy(left_ref, left, load_sems.at[1])
    right_load = pltpu.make_async_copy(right_ref, right, load_sems.at[2])
    psi_load.start()
    left_load.start()
    right_load.start()

    barrier = pltpu.get_barrier_semaphore()
    pl.semaphore_signal(barrier, inc=1, device_id={"sector": near}, device_id_type=MESH)
    for d in range(1, terms):
        pl.semaphore_signal(
            barrier, inc=1, device_id={"term": lax.rem(term + d, terms)}, device_id_type=MESH
        )

    @pl.when(has_far)
    def _():
        pl.semaphore_signal(barrier, inc=1, device_id={"sector": far}, device_id_type=MESH)

    psi_load.wait()
    index_row = lax.broadcasted_iota(jnp.int32, (block, block), 0)
    index_col = lax.broadcasted_iota(jnp.int32, (block, block), 1)
    reach = jnp.maximum(index_row, index_col)

    def mask(q, carry):
        nearby[q] = jnp.where(reach < sizes_ref[q], nearby[q], jnp.zeros((block, block), nearby.dtype))
        return carry

    lax.fori_loop(0, secs, mask, 0)
    pl.semaphore_wait(barrier, terms + has_far.astype(jnp.int32))

    near_copy = pltpu.make_async_remote_copy(
        nearby.at[pl.ds(0, secs)], nearby.at[pl.ds(secs, secs)], near_send, near_recv,
        device_id={"sector": near}, device_id_type=MESH,
    )

    def piece(i, mine):
        along_row, k = i % 2, i // 2
        odd_here = odd_row if along_row else odd_col
        if not mine:
            odd_here = 1 - odd_here
        return 2 * quarter * along_row + odd_here * quarter + k

    pieces = 2 * quarter

    def far_copy(i):
        q = piece(i, True)
        return pltpu.make_async_remote_copy(
            nearby.at[q], nearby.at[2 * secs + q], far_send.at[i], far_recv.at[i],
            device_id={"sector": far}, device_id_type=MESH,
        )

    def pass_copy(i, mine=True):
        q = piece(i, mine)
        return pltpu.make_async_remote_copy(
            nearby.at[2 * secs + q], nearby.at[2 * secs + q], pass_send.at[i], pass_recv.at[i],
            device_id={"term": row_mate if i % 2 else col_mate}, device_id_type=MESH,
        )

    @pl.when(has_far)
    def _():
        for i in range(pieces):
            far_copy(i).start()

    near_copy.start()

    @pl.when(has_far)
    def _():
        for i in range(pieces):
            far_copy(i).wait_recv()
            pass_copy(i).start()

    left_load.wait()
    right_load.wait()
    near_copy.wait()

    @pl.when(has_far)
    def _():
        for i in range(pieces):
            pass_copy(i, False).wait_recv()
        for i in range(pieces):
            far_copy(i).wait_send()
            pass_copy(i).wait_send()

    def visit(step, carry):
        for u in range(UNROLL):
            k = step * UNROLL + u
            code = order_ref[k]
            slot, src, tgt = code & 255, (code >> 8) & 255, code >> 16
            before = jnp.maximum(k - 1, 0)
            again = jnp.logical_and(k > 0, (order_ref[before] >> 16) == tgt)
            inner = jnp.dot(left[slot], nearby[src], preferred_element_type=jnp.float32).astype(
                jnp.bfloat16
            )
            here = lax.dot_general(
                inner, right[slot], (((1,), (1,)), ((), ())), preferred_element_type=jnp.float32
            )
            so_far = running[before]
            running[k] = here + jnp.where(again, so_far, jnp.zeros_like(so_far))
        return carry

    lax.fori_loop(0, slots // UNROLL, visit, 0)

    span = secs // RS_GROUPS

    def sum_copy(d, g):
        peer = lax.rem(term + d, terms)
        return pltpu.make_async_remote_copy(
            outgoing.at[peer, pl.ds(g * span, span)], incoming.at[d - 1, pl.ds(g * span, span)],
            sum_send.at[d - 1, g], sum_recv.at[d - 1, g],
            device_id={"term": peer}, device_id_type=MESH,
        )

    for g in range(RS_GROUPS):
        def finish(q, carry):
            end = ends_ref[q]
            start = jnp.where(q > 0, ends_ref[jnp.maximum(q - 1, 0)], 0)
            some = end > start
            at = jnp.maximum(end - 1, 0)
            for t in range(terms):
                total = running[at, t * rows : (t + 1) * rows, :]
                outgoing[t, q] = jnp.where(some, total, jnp.zeros_like(total)).astype(outgoing.dtype)
            total = running[at, pl.ds(pl.multiple_of(term * rows, rows), rows), :]
            own[q] = jnp.where(some, total, jnp.zeros_like(total))
            return carry

        lax.fori_loop(g * span, (g + 1) * span, finish, 0)
        for d in range(1, terms):
            sum_copy(d, g).start()

    for g in range(RS_GROUPS):
        for d in range(1, terms):
            sum_copy(d, g).wait_recv()

        def add(q, carry):
            total = own[q]
            for d in range(1, terms):
                total = total + incoming[d - 1, q].astype(jnp.float32)
            out_ref[q] = total
            return carry

        lax.fori_loop(g * span, (g + 1) * span, add, 0)
    for g in range(RS_GROUPS):
        for d in range(1, terms):
            sum_copy(d, g).wait_send()


def on_device(terms, groups, psi, sector_sizes, left_env, right_env, target, source, live_count):
    secs, block = psi.shape[0], psi.shape[1]
    slots = left_env.shape[0]
    rows = block // terms
    group = lax.axis_index("sector")
    tgt = target[:, 0] - group * secs
    src_group = source[:, 0] // secs
    place = jnp.where(src_group == group, 0, jnp.where(src_group == group + 1 - 2 * (group % 2), 1, 2))
    src = source[:, 0] - src_group * secs + place * secs
    slot = jnp.arange(slots, dtype=jnp.int32)
    tgt = jnp.where(slot < live_count[0, 0], tgt, secs)
    key = tgt * slots + slot
    rank = jnp.sum((key[None, :] < key[:, None]).astype(jnp.int32), axis=1)
    code = slot + src * 256 + tgt * 65536
    order = jnp.sum(jnp.where(rank[None, :] == slot[:, None], code[None, :], 0), axis=1)
    sec = jnp.arange(secs, dtype=jnp.int32)
    ends = jnp.sum((tgt[None, :] <= sec[:, None]).astype(jnp.int32), axis=1)
    pieces = 2 * (secs // 4)
    dma = pltpu.SemaphoreType.DMA
    total = pl.pallas_call(
        functools.partial(kernel, terms, groups),
        out_shape=jax.ShapeDtypeStruct((secs, rows, block), jnp.float32),
        in_specs=[pl.BlockSpec(memory_space=pltpu.SMEM)] * 3 + [pl.BlockSpec(memory_space=pl.ANY)] * 3,
        out_specs=pl.BlockSpec(memory_space=pltpu.VMEM),
        scratch_shapes=[
            pltpu.VMEM((3 * secs, block, block), jnp.bfloat16),
            pltpu.VMEM((slots, block, block), jnp.bfloat16),
            pltpu.VMEM((slots, block, block), jnp.bfloat16),
            pltpu.VMEM((slots, block, block), jnp.float32),
            pltpu.VMEM((terms, secs, rows, block), jnp.bfloat16),
            pltpu.VMEM((terms - 1, secs, rows, block), jnp.bfloat16),
            pltpu.VMEM((secs, rows, block), jnp.float32),
            dma((3,)), dma, dma, dma((pieces,)), dma((pieces,)), dma((pieces,)), dma((pieces,)),
            dma((terms - 1, RS_GROUPS)), dma((terms - 1, RS_GROUPS)),
        ],
        compiler_params=pltpu.CompilerParams(
            collective_id=0, has_side_effects=True, vmem_limit_bytes=60 * 1024 * 1024
        ),
    )(order, ends, sector_sizes, psi, left_env[:, 0], right_env[:, 0])
    index_row = lax.axis_index("term") * rows + jnp.arange(rows, dtype=jnp.int32)
    index_col = jnp.arange(block, dtype=jnp.int32)
    keep = (index_row[None, :, None] < sector_sizes[:, None, None]) & (
        index_col[None, None, :] < sector_sizes[:, None, None]
    )
    return jnp.where(keep, total, jnp.zeros_like(total))


def solution(mesh):
    placed = (
        P("sector", None, None),
        P("sector"),
        P("term", "sector", None, None),
        P("term", "sector", None, None),
        P("term", "sector"),
        P("term", "sector"),
        P("term", "sector"),
    )
    return jax.shard_map(
        functools.partial(on_device, mesh.shape["term"], mesh.shape["sector"]),
        mesh=mesh, in_specs=placed, out_specs=P("sector", "term", None), check_vma=False,
    )
```

```python
import functools
import math

import jax
import jax.numpy as jnp
from jax import lax
from jax.experimental import pallas as pl
from jax.experimental.pallas import tpu as pltpu
from jax.sharding import PartitionSpec as P

MESH = pl.DeviceIdType.MESH
SPLITS = 4
HALVES = 2
UNROLL = 4


def kernel(
    terms, groups,
    live_ref, sizes_ref, target_ref, source_ref, psi_ref, left_ref, right_ref,
    out_ref,
    nearby, left, right, inner, running, first_out, first_in, second_out, second_in, own, table, plan,
    load_sems, near_send, near_recv, far_send, far_recv, pass_send, pass_recv,
    first_send, first_recv, second_send, second_recv,
):
    secs, block = psi_ref.shape[0], psi_ref.shape[1]
    slots = left_ref.shape[0]
    rows = block // terms
    side = math.isqrt(terms)
    quarter = secs // 4
    group, term = lax.axis_index("sector"), lax.axis_index("term")
    odd = lax.rem(group, 2)
    near = group + 1 - 2 * odd
    far = group - 1 + 2 * odd
    has_far = jnp.logical_and(far >= 0, far < groups)
    col, row = lax.rem(term, side), lax.div(term, side)
    odd_col, odd_row = lax.rem(col, 2), lax.rem(row, 2)
    col_mate = term + 1 - 2 * odd_col
    row_mate = term + (1 - 2 * odd_row) * side

    psi_load = pltpu.make_async_copy(psi_ref, nearby.at[pl.ds(0, secs)], load_sems.at[0])
    left_load = pltpu.make_async_copy(left_ref, left, load_sems.at[1])
    right_load = pltpu.make_async_copy(right_ref, right, load_sems.at[2])
    psi_load.start()
    left_load.start()
    right_load.start()

    barrier = pltpu.get_barrier_semaphore()
    pl.semaphore_signal(barrier, inc=1, device_id={"sector": near}, device_id_type=MESH)
    for d in range(1, terms):
        pl.semaphore_signal(
            barrier, inc=1, device_id={"term": lax.rem(term + d, terms)}, device_id_type=MESH
        )

    @pl.when(has_far)
    def _():
        pl.semaphore_signal(barrier, inc=1, device_id={"sector": far}, device_id_type=MESH)

    psi_load.wait()
    index_row = lax.broadcasted_iota(jnp.int32, (block, block), 0)
    index_col = lax.broadcasted_iota(jnp.int32, (block, block), 1)
    reach = jnp.maximum(index_row, index_col)

    def mask(q, carry):
        nearby[q] = jnp.where(reach < sizes_ref[q], nearby[q], jnp.zeros((block, block), nearby.dtype))
        return carry

    lax.fori_loop(0, secs, mask, 0)
    pl.semaphore_wait(barrier, terms + has_far.astype(jnp.int32))

    near_copy = pltpu.make_async_remote_copy(
        nearby.at[pl.ds(0, secs)], nearby.at[pl.ds(secs, secs)], near_send, near_recv,
        device_id={"sector": near}, device_id_type=MESH,
    )

    def piece(i, mine):
        along_row, k = i % 2, i // 2
        odd_here = odd_row if along_row else odd_col
        if not mine:
            odd_here = 1 - odd_here
        return 2 * quarter * along_row + odd_here * quarter + k

    pieces = 2 * quarter

    def far_copy(i):
        q = piece(i, True)
        return pltpu.make_async_remote_copy(
            nearby.at[q], nearby.at[2 * secs + q], far_send.at[i], far_recv.at[i],
            device_id={"sector": far}, device_id_type=MESH,
        )

    def pass_copy(i, mine=True):
        q = piece(i, mine)
        return pltpu.make_async_remote_copy(
            nearby.at[2 * secs + q], nearby.at[2 * secs + q], pass_send.at[i], pass_recv.at[i],
            device_id={"term": row_mate if i % 2 else col_mate}, device_id_type=MESH,
        )

    @pl.when(has_far)
    def _():
        for i in range(pieces):
            far_copy(i).start()

    near_copy.start()

    lane = lax.broadcasted_iota(jnp.int32, (slots, slots), 1)
    line = lax.broadcasted_iota(jnp.int32, (slots, slots), 0)
    slot = lax.broadcasted_iota(jnp.int32, (1, slots), 1)

    def as_column(values):
        return jnp.sum(jnp.where(lane == line, values, 0), axis=1, keepdims=True)

    tgt = jnp.where(slot < live_ref[0, 0], target_ref[...] - group * secs, secs)
    from_own = source_ref[...] - group * secs
    from_near = source_ref[...] - near * secs
    from_far = source_ref[...] - far * secs
    src = jnp.where(
        (from_own >= 0) & (from_own < secs), from_own,
        jnp.where((from_near >= 0) & (from_near < secs), secs + from_near, 2 * secs + jnp.clip(from_far, 0, secs - 1)),
    )
    key = tgt * slots + slot
    rank = jnp.sum((key < as_column(key)).astype(jnp.int32), axis=1, keepdims=True)
    code = as_column(slot + src * 256 + tgt * 65536)
    table[...] = jnp.zeros_like(table)
    table[0:1, 0:slots] = jnp.sum(jnp.where(rank == lane, code, 0), axis=0, keepdims=True)
    sec = lax.broadcasted_iota(jnp.int32, (slots, 128), 1)
    table[1:2, :] = jnp.sum((as_column(tgt) <= sec).astype(jnp.int32), axis=0, keepdims=True)
    plan_load = pltpu.make_async_copy(table, plan, load_sems.at[3])
    plan_load.start()
    plan_load.wait()

    @pl.when(has_far)
    def _():
        for i in range(pieces):
            far_copy(i).wait_recv()
            pass_copy(i).start()

    left_load.wait()
    right_load.wait()
    near_copy.wait()

    @pl.when(has_far)
    def _():
        for i in range(pieces):
            pass_copy(i, False).wait_recv()
        for i in range(pieces):
            far_copy(i).wait_send()
            pass_copy(i).wait_send()

    def multiply(step, carry):
        for u in range(UNROLL):
            k = step * UNROLL + u
            code = plan[0, k]
            inner[k] = jnp.dot(
                left[code & 255], nearby[(code >> 8) & 255], preferred_element_type=jnp.float32
            ).astype(jnp.bfloat16)
        return carry

    lax.fori_loop(0, slots // UNROLL, multiply, 0)

    width = block // HALVES
    span = secs // SPLITS

    def places(part):
        return (row, col) if part % 2 else (col, row)

    def term_at(part, first, second):
        return first * side + second if part % 2 else second * side + first

    def first_copy(half, part, d):
        first, second = places(part)
        to = lax.rem(first + d, side)
        return pltpu.make_async_remote_copy(
            first_out.at[half, part, to], first_in.at[half, part, d - 1],
            first_send.at[half, part, d - 1], first_recv.at[half, part, d - 1],
            device_id={"term": term_at(part, to, second)}, device_id_type=MESH,
        )

    def second_copy(half, part, d):
        first, second = places(part)
        to = lax.rem(second + d, side)
        return pltpu.make_async_remote_copy(
            second_out.at[half, part, d - 1], second_in.at[half, part, d - 1],
            second_send.at[half, part, d - 1], second_recv.at[half, part, d - 1],
            device_id={"term": term_at(part, first, to)}, device_id_type=MESH,
        )

    def summed(half, q, place):
        end = plan[1, q]
        start = jnp.where(q > 0, plan[1, jnp.maximum(q - 1, 0)], 0)
        at = pl.multiple_of(place * rows, rows)
        total = running[half, jnp.maximum(end - 1, 0), pl.ds(at, rows), :]
        return jnp.where(end > start, total, jnp.zeros_like(total))

    for half in range(HALVES):
        def visit(step, carry):
            for u in range(UNROLL):
                k = step * UNROLL + u
                code = plan[0, k]
                before = jnp.maximum(k - 1, 0)
                again = jnp.logical_and(k > 0, (plan[0, before] >> 16) == (code >> 16))
                here = lax.dot_general(
                    inner[k], right[code & 255, half * width : (half + 1) * width, :],
                    (((1,), (1,)), ((), ())), preferred_element_type=jnp.float32,
                )
                so_far = running[half, before]
                running[half, k] = here + jnp.where(again, so_far, jnp.zeros_like(so_far))
            return carry

        lax.fori_loop(0, slots // UNROLL, visit, 0)

        for part in range(SPLITS):
            first, second = places(part)

            def give(i, carry):
                for a in range(side):
                    for b in range(side):
                        first_out[half, part, a, b, i] = summed(
                            half, part * span + i, term_at(part, a, b)
                        ).astype(first_out.dtype)
                return carry

            lax.fori_loop(0, span, give, 0)
            for d in range(1, side):
                first_copy(half, part, d).start()

    for half in range(HALVES):
        for part in range(SPLITS):
            first, second = places(part)
            for d in range(1, side):
                first_copy(half, part, d).wait_recv()

            def pass_on(i, carry):
                def partial_sum(b):
                    total = summed(half, part * span + i, term_at(part, first, b))
                    for d in range(1, side):
                        total = total + first_in[half, part, d - 1, b, i].astype(jnp.float32)
                    return total

                for d in range(1, side):
                    second_out[half, part, d - 1, i] = partial_sum(lax.rem(second + d, side)).astype(
                        second_out.dtype
                    )
                own[half, part * span + i] = partial_sum(second)
                return carry

            lax.fori_loop(0, span, pass_on, 0)
            for d in range(1, side):
                second_copy(half, part, d).start()

    for half in range(HALVES):
        columns = slice(half * width, (half + 1) * width)
        for part in range(SPLITS):
            for d in range(1, side):
                second_copy(half, part, d).wait_recv()

            def add(i, carry):
                total = own[half, part * span + i]
                for d in range(1, side):
                    total = total + second_in[half, part, d - 1, i].astype(jnp.float32)
                out_ref[part * span + i, :, columns] = total
                return carry

            lax.fori_loop(0, span, add, 0)
    for half in range(HALVES):
        for part in range(SPLITS):
            for d in range(1, side):
                first_copy(half, part, d).wait_send()
                second_copy(half, part, d).wait_send()


def on_device(terms, groups, psi, sector_sizes, left_env, right_env, target, source, live_count):
    secs, block = psi.shape[0], psi.shape[1]
    slots = left_env.shape[0]
    rows, side, span, width = block // terms, math.isqrt(terms), secs // SPLITS, block // HALVES
    pieces = 2 * (secs // 4)
    dma = pltpu.SemaphoreType.DMA
    smem, vmem, here = (pl.BlockSpec(memory_space=m) for m in (pltpu.SMEM, pltpu.VMEM, pl.ANY))
    total = pl.pallas_call(
        functools.partial(kernel, terms, groups),
        out_shape=jax.ShapeDtypeStruct((secs, rows, block), jnp.float32),
        in_specs=[smem, smem, vmem, vmem, here, here, here],
        out_specs=vmem,
        scratch_shapes=[
            pltpu.VMEM((3 * secs, block, block), jnp.bfloat16),
            pltpu.VMEM((slots, block, block), jnp.bfloat16),
            pltpu.VMEM((slots, block, block), jnp.bfloat16),
            pltpu.VMEM((slots, block, block), jnp.bfloat16),
            pltpu.VMEM((HALVES, slots, block, width), jnp.float32),
            pltpu.VMEM((HALVES, SPLITS, side, side, span, rows, width), jnp.bfloat16),
            pltpu.VMEM((HALVES, SPLITS, side - 1, side, span, rows, width), jnp.bfloat16),
            pltpu.VMEM((HALVES, SPLITS, side - 1, span, rows, width), jnp.bfloat16),
            pltpu.VMEM((HALVES, SPLITS, side - 1, span, rows, width), jnp.bfloat16),
            pltpu.VMEM((HALVES, secs, rows, width), jnp.float32),
            pltpu.VMEM((8, 128), jnp.int32),
            pltpu.SMEM((8, 128), jnp.int32),
            dma((4,)), dma, dma, dma((pieces,)), dma((pieces,)), dma((pieces,)), dma((pieces,)),
            *[dma((HALVES, SPLITS, side - 1))] * 4,
        ],
        compiler_params=pltpu.CompilerParams(
            collective_id=0, has_side_effects=True, vmem_limit_bytes=54 * 1024 * 1024
        ),
    )(
        live_count, sector_sizes, target.reshape(1, slots), source.reshape(1, slots),
        psi, left_env[:, 0], right_env[:, 0],
    )
    index_row = lax.axis_index("term") * rows + jnp.arange(rows, dtype=jnp.int32)
    index_col = jnp.arange(block, dtype=jnp.int32)
    keep = (index_row[None, :, None] < sector_sizes[:, None, None]) & (
        index_col[None, None, :] < sector_sizes[:, None, None]
    )
    return jnp.where(keep, total, jnp.zeros_like(total))


def solution(mesh):
    placed = (
        P("sector", None, None),
        P("sector"),
        P("term", "sector", None, None),
        P("term", "sector", None, None),
        P("term", "sector"),
        P("term", "sector"),
        P("term", "sector"),
    )
    return jax.shard_map(
        functools.partial(on_device, mesh.shape["term"], mesh.shape["sector"]),
        mesh=mesh, in_specs=placed, out_specs=P("sector", "term", None), check_vma=False,
    )
```

```python
import functools
import math

import jax
import jax.numpy as jnp
from jax import lax
from jax.experimental import pallas as pl
from jax.experimental.pallas import tpu as pltpu
from jax.sharding import PartitionSpec as P

MESH = pl.DeviceIdType.MESH
SPLITS = 4
HALVES = 2
UNROLL = 16


def kernel(
    terms, groups,
    live_ref, sizes_ref, target_ref, source_ref, psi_ref, left_ref, right_ref,
    out_ref,
    nearby, left, right, inner, running, first_out, first_in, second_out, second_in, own, table, plan,
    load_sems, near_send, near_recv, far_send, far_recv, pass_send, pass_recv,
    first_send, first_recv, second_send, second_recv,
):
    secs, block = psi_ref.shape[0], psi_ref.shape[1]
    slots = left_ref.shape[0]
    rows = block // terms
    side = math.isqrt(terms)
    quarter = secs // 4
    group, term = lax.axis_index("sector"), lax.axis_index("term")
    odd = lax.rem(group, 2)
    near = group + 1 - 2 * odd
    far = group - 1 + 2 * odd
    has_far = jnp.logical_and(far >= 0, far < groups)
    col, row = lax.rem(term, side), lax.div(term, side)
    odd_col, odd_row = lax.rem(col, 2), lax.rem(row, 2)
    col_mate = term + 1 - 2 * odd_col
    row_mate = term + (1 - 2 * odd_row) * side

    psi_load = pltpu.make_async_copy(psi_ref, nearby.at[pl.ds(0, secs)], load_sems.at[0])
    left_load = pltpu.make_async_copy(left_ref, left, load_sems.at[1])
    right_load = pltpu.make_async_copy(right_ref, right, load_sems.at[2])
    psi_load.start()
    left_load.start()
    right_load.start()

    barrier = pltpu.get_barrier_semaphore()
    pl.semaphore_signal(barrier, inc=1, device_id={"sector": near}, device_id_type=MESH)
    for d in range(1, terms):
        pl.semaphore_signal(
            barrier, inc=1, device_id={"term": lax.rem(term + d, terms)}, device_id_type=MESH
        )

    @pl.when(has_far)
    def _():
        pl.semaphore_signal(barrier, inc=1, device_id={"sector": far}, device_id_type=MESH)

    psi_load.wait()
    index_row = lax.broadcasted_iota(jnp.int32, (block, block), 0)
    index_col = lax.broadcasted_iota(jnp.int32, (block, block), 1)
    reach = jnp.maximum(index_row, index_col)

    def mask(q, carry):
        nearby[q] = jnp.where(reach < sizes_ref[q], nearby[q], jnp.zeros((block, block), nearby.dtype))
        return carry

    lax.fori_loop(0, secs, mask, 0, unroll=4)
    pl.semaphore_wait(barrier, terms + has_far.astype(jnp.int32))

    near_copy = pltpu.make_async_remote_copy(
        nearby.at[pl.ds(0, secs)], nearby.at[pl.ds(secs, secs)], near_send, near_recv,
        device_id={"sector": near}, device_id_type=MESH,
    )

    def piece(i, mine):
        along_row, k = i % 2, i // 2
        odd_here = odd_row if along_row else odd_col
        if not mine:
            odd_here = 1 - odd_here
        return 2 * quarter * along_row + odd_here * quarter + k

    pieces = 2 * quarter

    def far_copy(i):
        q = piece(i, True)
        return pltpu.make_async_remote_copy(
            nearby.at[q], nearby.at[2 * secs + q], far_send.at[i], far_recv.at[i],
            device_id={"sector": far}, device_id_type=MESH,
        )

    def pass_copy(i, mine=True):
        q = piece(i, mine)
        return pltpu.make_async_remote_copy(
            nearby.at[2 * secs + q], nearby.at[2 * secs + q], pass_send.at[i], pass_recv.at[i],
            device_id={"term": row_mate if i % 2 else col_mate}, device_id_type=MESH,
        )

    @pl.when(has_far)
    def _():
        for i in range(pieces):
            far_copy(i).start()

    near_copy.start()

    lane = lax.broadcasted_iota(jnp.int32, (slots, slots), 1)
    line = lax.broadcasted_iota(jnp.int32, (slots, slots), 0)
    slot = lax.broadcasted_iota(jnp.int32, (1, slots), 1)

    def as_column(values):
        return jnp.sum(jnp.where(lane == line, values, 0), axis=1, keepdims=True)

    tgt = jnp.where(slot < live_ref[0, 0], target_ref[...] - group * secs, secs)
    from_own = source_ref[...] - group * secs
    from_near = source_ref[...] - near * secs
    from_far = source_ref[...] - far * secs
    src = jnp.where(
        (from_own >= 0) & (from_own < secs), from_own,
        jnp.where((from_near >= 0) & (from_near < secs), secs + from_near, 2 * secs + jnp.clip(from_far, 0, secs - 1)),
    )
    key = tgt * slots + slot
    rank = jnp.sum((key < as_column(key)).astype(jnp.int32), axis=1, keepdims=True)
    code = as_column(slot + src * 256 + tgt * 65536)
    table[...] = jnp.zeros_like(table)
    table[0:1, 0:slots] = jnp.sum(jnp.where(rank == lane, code, 0), axis=0, keepdims=True)
    sec = lax.broadcasted_iota(jnp.int32, (slots, 128), 1)
    table[1:2, :] = jnp.sum((as_column(tgt) <= sec).astype(jnp.int32), axis=0, keepdims=True)
    plan_load = pltpu.make_async_copy(table, plan, load_sems.at[3])
    plan_load.start()
    plan_load.wait()

    @pl.when(has_far)
    def _():
        for i in range(pieces):
            far_copy(i).wait_recv()
            pass_copy(i).start()

    left_load.wait()
    right_load.wait()
    near_copy.wait()

    @pl.when(has_far)
    def _():
        for i in range(pieces):
            pass_copy(i, False).wait_recv()
        for i in range(pieces):
            far_copy(i).wait_send()
            pass_copy(i).wait_send()

    def multiply(step, carry):
        for u in range(UNROLL):
            k = step * UNROLL + u
            code = plan[0, k]
            inner[k] = jnp.dot(
                left[code & 255], nearby[(code >> 8) & 255], preferred_element_type=jnp.float32
            ).astype(jnp.bfloat16)
        return carry

    lax.fori_loop(0, slots // UNROLL, multiply, 0)

    width = block // HALVES
    span = secs // SPLITS

    def places(part):
        return (row, col) if part % 2 else (col, row)

    def term_at(part, first, second):
        return first * side + second if part % 2 else second * side + first

    def first_copy(half, part, d):
        first, second = places(part)
        to = lax.rem(first + d, side)
        return pltpu.make_async_remote_copy(
            first_out.at[half, part, to], first_in.at[half, part, d - 1],
            first_send.at[half, part, d - 1], first_recv.at[half, part, d - 1],
            device_id={"term": term_at(part, to, second)}, device_id_type=MESH,
        )

    def second_copy(half, part, d):
        first, second = places(part)
        to = lax.rem(second + d, side)
        return pltpu.make_async_remote_copy(
            second_out.at[half, part, d - 1], second_in.at[half, part, d - 1],
            second_send.at[half, part, d - 1], second_recv.at[half, part, d - 1],
            device_id={"term": term_at(part, first, to)}, device_id_type=MESH,
        )

    def summed(half, q, place):
        end = plan[1, q]
        start = jnp.where(q > 0, plan[1, jnp.maximum(q - 1, 0)], 0)
        at = pl.multiple_of(place * rows, rows)
        total = running[half, jnp.maximum(end - 1, 0), pl.ds(at, rows), :]
        return jnp.where(end > start, total, jnp.zeros_like(total))

    for half in range(HALVES):
        def visit(step, carry):
            for u in range(UNROLL):
                k = step * UNROLL + u
                code = plan[0, k]
                before = jnp.maximum(k - 1, 0)
                again = jnp.logical_and(k > 0, (plan[0, before] >> 16) == (code >> 16))
                here = lax.dot_general(
                    inner[k], right[code & 255, half * width : (half + 1) * width, :],
                    (((1,), (1,)), ((), ())), preferred_element_type=jnp.float32,
                )
                so_far = running[half, before]
                running[half, k] = here + jnp.where(again, so_far, jnp.zeros_like(so_far))
            return carry

        lax.fori_loop(0, slots // UNROLL, visit, 0)

        for part in range(SPLITS):
            first, second = places(part)

            def give(i, carry):
                for a in range(side):
                    for b in range(side):
                        first_out[half, part, a, b, i] = summed(
                            half, part * span + i, term_at(part, a, b)
                        ).astype(first_out.dtype)
                return carry

            lax.fori_loop(0, span, give, 0, unroll=True)
            for d in range(1, side):
                first_copy(half, part, d).start()

    for half in range(HALVES):
        for part in range(SPLITS):
            first, second = places(part)
            for d in range(1, side):
                first_copy(half, part, d).wait_recv()

            def pass_on(i, carry):
                def partial_sum(b):
                    total = summed(half, part * span + i, term_at(part, first, b))
                    for d in range(1, side):
                        total = total + first_in[half, part, d - 1, b, i].astype(jnp.float32)
                    return total

                for d in range(1, side):
                    second_out[half, part, d - 1, i] = partial_sum(lax.rem(second + d, side)).astype(
                        second_out.dtype
                    )
                own[half, part * span + i] = partial_sum(second)
                return carry

            lax.fori_loop(0, span, pass_on, 0, unroll=True)
            for d in range(1, side):
                second_copy(half, part, d).start()

    kept_row = lax.broadcasted_iota(jnp.int32, (rows, width), 0) + term * rows
    kept_col = lax.broadcasted_iota(jnp.int32, (rows, width), 1)
    for half in range(HALVES):
        columns = slice(half * width, (half + 1) * width)
        for part in range(SPLITS):
            for d in range(1, side):
                second_copy(half, part, d).wait_recv()

            def add(i, carry):
                total = own[half, part * span + i]
                for d in range(1, side):
                    total = total + second_in[half, part, d - 1, i].astype(jnp.float32)
                live = sizes_ref[part * span + i]
                keep = (kept_row < live) & (kept_col < live - half * width)
                out_ref[part * span + i, :, columns] = jnp.where(keep, total, jnp.zeros_like(total))
                return carry

            lax.fori_loop(0, span, add, 0, unroll=True)
    for half in range(HALVES):
        for part in range(SPLITS):
            for d in range(1, side):
                first_copy(half, part, d).wait_send()
                second_copy(half, part, d).wait_send()


def on_device(terms, groups, psi, sector_sizes, left_env, right_env, target, source, live_count):
    secs, block = psi.shape[0], psi.shape[1]
    slots = left_env.shape[0]
    rows, side, span, width = block // terms, math.isqrt(terms), secs // SPLITS, block // HALVES
    pieces = 2 * (secs // 4)
    dma = pltpu.SemaphoreType.DMA
    smem, vmem, here = (pl.BlockSpec(memory_space=m) for m in (pltpu.SMEM, pltpu.VMEM, pl.ANY))
    return pl.pallas_call(
        functools.partial(kernel, terms, groups),
        out_shape=jax.ShapeDtypeStruct((secs, rows, block), jnp.float32),
        in_specs=[smem, smem, vmem, vmem, here, here, here],
        out_specs=vmem,
        scratch_shapes=[
            pltpu.VMEM((3 * secs, block, block), jnp.bfloat16),
            pltpu.VMEM((slots, block, block), jnp.bfloat16),
            pltpu.VMEM((slots, block, block), jnp.bfloat16),
            pltpu.VMEM((slots, block, block), jnp.bfloat16),
            pltpu.VMEM((HALVES, slots, block, width), jnp.float32),
            pltpu.VMEM((HALVES, SPLITS, side, side, span, rows, width), jnp.bfloat16),
            pltpu.VMEM((HALVES, SPLITS, side - 1, side, span, rows, width), jnp.bfloat16),
            pltpu.VMEM((HALVES, SPLITS, side - 1, span, rows, width), jnp.bfloat16),
            pltpu.VMEM((HALVES, SPLITS, side - 1, span, rows, width), jnp.bfloat16),
            pltpu.VMEM((HALVES, secs, rows, width), jnp.float32),
            pltpu.VMEM((8, 128), jnp.int32),
            pltpu.SMEM((8, 128), jnp.int32),
            dma((4,)), dma, dma, dma((pieces,)), dma((pieces,)), dma((pieces,)), dma((pieces,)),
            *[dma((HALVES, SPLITS, side - 1))] * 4,
        ],
        compiler_params=pltpu.CompilerParams(
            collective_id=0, has_side_effects=True, vmem_limit_bytes=52 * 1024 * 1024
        ),
    )(
        live_count, sector_sizes, target.reshape(1, slots), source.reshape(1, slots),
        psi, left_env[:, 0], right_env[:, 0],
    )


def solution(mesh):
    placed = (
        P("sector", None, None),
        P("sector"),
        P("term", "sector", None, None),
        P("term", "sector", None, None),
        P("term", "sector"),
        P("term", "sector"),
        P("term", "sector"),
    )
    return jax.shard_map(
        functools.partial(on_device, mesh.shape["term"], mesh.shape["sector"]),
        mesh=mesh, in_specs=placed, out_specs=P("sector", "term", None), check_vma=False,
    )
```

```python
import functools
import math

import jax
import jax.numpy as jnp
from jax import lax
from jax.experimental import pallas as pl
from jax.experimental.pallas import tpu as pltpu
from jax.sharding import PartitionSpec as P

MESH = pl.DeviceIdType.MESH
SPLITS = 4
DIRECT = 1
HALVES = 2
UNROLL = 16


def kernel(
    terms, groups,
    live_ref, sizes_ref, target_ref, source_ref, psi_ref, left_ref, right_ref,
    out_ref,
    nearby, left, right, inner, running, first_out, first_in, second_out, second_in, own, table, plan,
    load_sems, near_send, near_recv, far_send, far_recv, pass_send, pass_recv,
    first_send, first_recv, second_send, second_recv,
):
    secs, block = psi_ref.shape[0], psi_ref.shape[1]
    slots = left_ref.shape[0]
    rows = block // terms
    side = math.isqrt(terms)
    quarter = secs // 4
    group, term = lax.axis_index("sector"), lax.axis_index("term")
    odd = lax.rem(group, 2)
    near = group + 1 - 2 * odd
    far = group - 1 + 2 * odd
    has_far = jnp.logical_and(far >= 0, far < groups)
    col, row = lax.rem(term, side), lax.div(term, side)
    odd_col, odd_row = lax.rem(col, 2), lax.rem(row, 2)
    col_mate = term + 1 - 2 * odd_col
    row_mate = term + (1 - 2 * odd_row) * side

    psi_load = pltpu.make_async_copy(psi_ref, nearby.at[pl.ds(0, secs)], load_sems.at[0])
    left_load = pltpu.make_async_copy(left_ref, left, load_sems.at[1])
    right_load = pltpu.make_async_copy(right_ref, right, load_sems.at[2])
    psi_load.start()
    left_load.start()
    right_load.start()

    barrier = pltpu.get_barrier_semaphore()
    pl.semaphore_signal(barrier, inc=1, device_id={"sector": near}, device_id_type=MESH)
    for d in range(1, terms):
        pl.semaphore_signal(
            barrier, inc=1, device_id={"term": lax.rem(term + d, terms)}, device_id_type=MESH
        )

    @pl.when(has_far)
    def _():
        pl.semaphore_signal(barrier, inc=1, device_id={"sector": far}, device_id_type=MESH)

    psi_load.wait()
    index_row = lax.broadcasted_iota(jnp.int32, (block, block), 0)
    index_col = lax.broadcasted_iota(jnp.int32, (block, block), 1)
    reach = jnp.maximum(index_row, index_col)

    def mask(q, carry):
        nearby[q] = jnp.where(reach < sizes_ref[q], nearby[q], jnp.zeros((block, block), nearby.dtype))
        return carry

    lax.fori_loop(0, secs, mask, 0, unroll=4)
    pl.semaphore_wait(barrier, terms + has_far.astype(jnp.int32))

    near_copy = pltpu.make_async_remote_copy(
        nearby.at[pl.ds(0, secs)], nearby.at[pl.ds(secs, secs)], near_send, near_recv,
        device_id={"sector": near}, device_id_type=MESH,
    )

    def piece(i, mine):
        along_row, k = i % 2, i // 2
        odd_here = odd_row if along_row else odd_col
        if not mine:
            odd_here = 1 - odd_here
        return 2 * quarter * along_row + odd_here * quarter + k

    pieces = 2 * quarter
    direct = 2 * DIRECT
    passed = pieces - direct

    def straight_copy(i):
        q = piece(passed + i, False)
        return pltpu.make_async_remote_copy(
            nearby.at[q], nearby.at[2 * secs + q], far_send.at[pieces + i], far_recv.at[pieces + i],
            device_id={"sector": far}, device_id_type=MESH,
        )

    def far_copy(i):
        q = piece(i, True)
        return pltpu.make_async_remote_copy(
            nearby.at[q], nearby.at[2 * secs + q], far_send.at[i], far_recv.at[i],
            device_id={"sector": far}, device_id_type=MESH,
        )

    def pass_copy(i, mine=True):
        q = piece(i, mine)
        return pltpu.make_async_remote_copy(
            nearby.at[2 * secs + q], nearby.at[2 * secs + q], pass_send.at[i], pass_recv.at[i],
            device_id={"term": row_mate if i % 2 else col_mate}, device_id_type=MESH,
        )

    @pl.when(has_far)
    def _():
        for i in range(pieces):
            far_copy(i).start()
        for i in range(direct):
            straight_copy(i).start()

    near_copy.start()

    lane = lax.broadcasted_iota(jnp.int32, (slots, slots), 1)
    line = lax.broadcasted_iota(jnp.int32, (slots, slots), 0)
    slot = lax.broadcasted_iota(jnp.int32, (1, slots), 1)

    def as_column(values):
        return jnp.sum(jnp.where(lane == line, values, 0), axis=1, keepdims=True)

    tgt = jnp.where(slot < live_ref[0, 0], target_ref[...] - group * secs, secs)
    from_own = source_ref[...] - group * secs
    from_near = source_ref[...] - near * secs
    from_far = source_ref[...] - far * secs
    src = jnp.where(
        (from_own >= 0) & (from_own < secs), from_own,
        jnp.where((from_near >= 0) & (from_near < secs), secs + from_near, 2 * secs + jnp.clip(from_far, 0, secs - 1)),
    )
    key = tgt * slots + slot
    rank = jnp.sum((key < as_column(key)).astype(jnp.int32), axis=1, keepdims=True)
    code = as_column(slot + src * 256 + tgt * 65536)
    table[...] = jnp.zeros_like(table)
    table[0:1, 0:slots] = jnp.sum(jnp.where(rank == lane, code, 0), axis=0, keepdims=True)
    sec = lax.broadcasted_iota(jnp.int32, (slots, 128), 1)
    table[1:2, :] = jnp.sum((as_column(tgt) <= sec).astype(jnp.int32), axis=0, keepdims=True)
    plan_load = pltpu.make_async_copy(table, plan, load_sems.at[3])
    plan_load.start()
    plan_load.wait()

    @pl.when(has_far)
    def _():
        for i in range(pieces):
            far_copy(i).wait_recv()
            if i < passed:
                pass_copy(i).start()

    left_load.wait()
    right_load.wait()
    near_copy.wait()

    @pl.when(has_far)
    def _():
        for i in range(passed):
            pass_copy(i, False).wait_recv()
            pass_copy(i).wait_send()
        for i in range(direct):
            straight_copy(i).wait()
        for i in range(pieces):
            far_copy(i).wait_send()

    def multiply(step, carry):
        for u in range(UNROLL):
            k = step * UNROLL + u
            code = plan[0, k]
            inner[k] = jnp.dot(
                left[code & 255], nearby[(code >> 8) & 255], preferred_element_type=jnp.float32
            ).astype(jnp.bfloat16)
        return carry

    lax.fori_loop(0, slots // UNROLL, multiply, 0)

    width = block // HALVES
    span = secs // SPLITS

    def places(part):
        return (row, col) if part % 2 else (col, row)

    def term_at(part, first, second):
        return first * side + second if part % 2 else second * side + first

    def first_copy(half, part, d):
        first, second = places(part)
        to = lax.rem(first + d, side)
        return pltpu.make_async_remote_copy(
            first_out.at[half, part, to], first_in.at[half, part, d - 1],
            first_send.at[half, part, d - 1], first_recv.at[half, part, d - 1],
            device_id={"term": term_at(part, to, second)}, device_id_type=MESH,
        )

    def second_copy(half, part, d):
        first, second = places(part)
        to = lax.rem(second + d, side)
        return pltpu.make_async_remote_copy(
            second_out.at[half, part, d - 1], second_in.at[half, part, d - 1],
            second_send.at[half, part, d - 1], second_recv.at[half, part, d - 1],
            device_id={"term": term_at(part, first, to)}, device_id_type=MESH,
        )

    def summed(half, q, place):
        end = plan[1, q]
        start = jnp.where(q > 0, plan[1, jnp.maximum(q - 1, 0)], 0)
        at = pl.multiple_of(place * rows, rows)
        total = running[half, jnp.maximum(end - 1, 0), pl.ds(at, rows), :]
        return jnp.where(end > start, total, jnp.zeros_like(total))

    for half in range(HALVES):
        def visit(step, carry):
            for u in range(UNROLL):
                k = step * UNROLL + u
                code = plan[0, k]
                before = jnp.maximum(k - 1, 0)
                again = jnp.logical_and(k > 0, (plan[0, before] >> 16) == (code >> 16))
                here = lax.dot_general(
                    inner[k], right[code & 255, half * width : (half + 1) * width, :],
                    (((1,), (1,)), ((), ())), preferred_element_type=jnp.float32,
                )
                so_far = running[half, before]
                running[half, k] = here + jnp.where(again, so_far, jnp.zeros_like(so_far))
            return carry

        lax.fori_loop(0, slots // UNROLL, visit, 0)

        for part in range(SPLITS):
            first, second = places(part)

            def give(i, carry):
                for a in range(side):
                    for b in range(side):
                        first_out[half, part, a, b, i] = summed(
                            half, part * span + i, term_at(part, a, b)
                        ).astype(first_out.dtype)
                return carry

            lax.fori_loop(0, span, give, 0, unroll=True)
            for d in range(1, side):
                first_copy(half, part, d).start()

    for half in range(HALVES):
        for part in range(SPLITS):
            first, second = places(part)
            for d in range(1, side):
                first_copy(half, part, d).wait_recv()

            def pass_on(i, carry):
                def partial_sum(b):
                    total = summed(half, part * span + i, term_at(part, first, b))
                    for d in range(1, side):
                        total = total + first_in[half, part, d - 1, b, i].astype(jnp.float32)
                    return total

                for d in range(1, side):
                    second_out[half, part, d - 1, i] = partial_sum(lax.rem(second + d, side)).astype(
                        second_out.dtype
                    )
                own[half, part * span + i] = partial_sum(second)
                return carry

            lax.fori_loop(0, span, pass_on, 0, unroll=True)
            for d in range(1, side):
                second_copy(half, part, d).start()

    kept_row = lax.broadcasted_iota(jnp.int32, (rows, width), 0) + term * rows
    kept_col = lax.broadcasted_iota(jnp.int32, (rows, width), 1)
    for half in range(HALVES):
        columns = slice(half * width, (half + 1) * width)
        for part in range(SPLITS):
            for d in range(1, side):
                second_copy(half, part, d).wait_recv()

            def add(i, carry):
                total = own[half, part * span + i]
                for d in range(1, side):
                    total = total + second_in[half, part, d - 1, i].astype(jnp.float32)
                live = sizes_ref[part * span + i]
                keep = (kept_row < live) & (kept_col < live - half * width)
                out_ref[part * span + i, :, columns] = jnp.where(keep, total, jnp.zeros_like(total))
                return carry

            lax.fori_loop(0, span, add, 0, unroll=True)
    for half in range(HALVES):
        for part in range(SPLITS):
            for d in range(1, side):
                first_copy(half, part, d).wait_send()
                second_copy(half, part, d).wait_send()


def on_device(terms, groups, psi, sector_sizes, left_env, right_env, target, source, live_count):
    secs, block = psi.shape[0], psi.shape[1]
    slots = left_env.shape[0]
    rows, side, span, width = block // terms, math.isqrt(terms), secs // SPLITS, block // HALVES
    pieces = 2 * (secs // 4)
    dma = pltpu.SemaphoreType.DMA
    smem, vmem, here = (pl.BlockSpec(memory_space=m) for m in (pltpu.SMEM, pltpu.VMEM, pl.ANY))
    return pl.pallas_call(
        functools.partial(kernel, terms, groups),
        out_shape=jax.ShapeDtypeStruct((secs, rows, block), jnp.float32),
        in_specs=[smem, smem, vmem, vmem, here, here, here],
        out_specs=vmem,
        scratch_shapes=[
            pltpu.VMEM((3 * secs, block, block), jnp.bfloat16),
            pltpu.VMEM((slots, block, block), jnp.bfloat16),
            pltpu.VMEM((slots, block, block), jnp.bfloat16),
            pltpu.VMEM((slots, block, block), jnp.bfloat16),
            pltpu.VMEM((HALVES, slots, block, width), jnp.float32),
            pltpu.VMEM((HALVES, SPLITS, side, side, span, rows, width), jnp.bfloat16),
            pltpu.VMEM((HALVES, SPLITS, side - 1, side, span, rows, width), jnp.bfloat16),
            pltpu.VMEM((HALVES, SPLITS, side - 1, span, rows, width), jnp.bfloat16),
            pltpu.VMEM((HALVES, SPLITS, side - 1, span, rows, width), jnp.bfloat16),
            pltpu.VMEM((HALVES, secs, rows, width), jnp.float32),
            pltpu.VMEM((8, 128), jnp.int32),
            pltpu.SMEM((8, 128), jnp.int32),
            dma((4,)), dma, dma, dma((pieces + 2 * DIRECT,)), dma((pieces + 2 * DIRECT,)), dma((pieces,)), dma((pieces,)),
            *[dma((HALVES, SPLITS, side - 1))] * 4,
        ],
        compiler_params=pltpu.CompilerParams(
            collective_id=0, has_side_effects=True, vmem_limit_bytes=52 * 1024 * 1024
        ),
    )(
        live_count, sector_sizes, target.reshape(1, slots), source.reshape(1, slots),
        psi, left_env[:, 0], right_env[:, 0],
    )


def solution(mesh):
    placed = (
        P("sector", None, None),
        P("sector"),
        P("term", "sector", None, None),
        P("term", "sector", None, None),
        P("term", "sector"),
        P("term", "sector"),
        P("term", "sector"),
    )
    return jax.shard_map(
        functools.partial(on_device, mesh.shape["term"], mesh.shape["sector"]),
        mesh=mesh, in_specs=placed, out_specs=P("sector", "term", None), check_vma=False,
    )
```
